32 devices in a mesh: blk: 8 (over z, y), rhs: 4 (over x, core).
Axes of the slice: x: 2, y: 2, z: 4, core: 2. Of those that a mesh axis runs over, the one named last changes fastest.
Arguments:
- rhs: float32 [8, 8, 8, 256, 128], P(None, None, 'blk', 'rhs'), parts along dimension 3, may hold values from -6 to 6
- lower_tiles: bfloat16 [8, 8, 8, 3, 128, 128], P(None, None, 'blk'), may hold values from -0.25 to 0.25
- lower_block_columns: int32 [8, 8, 8, 3], P(None, None, 'blk'), may hold values from 0 to 511, as said below
- upper_tiles: bfloat16 [8, 8, 8, 3, 128, 128], P(None, None, 'blk'), may hold values from -0.25 to 0.25
- upper_cols: int32 [8, 8, 8, 3], P(None, None, 'blk'), may hold values from 0 to 511, as said below
- diag_inverse: bfloat16 [8, 8, 8, 128, 128], P(None, None, 'blk')
Outputs:
- solution: bfloat16 [8, 8, 8, 256, 128], P(None, None, 'blk', 'rhs'), parts along dimension 3
The draws below stay inside these ranges and needn't reach their ends.
There are 4 independent parts, one for each index of `rhs`. The reference program is written for one: setup_inputs(seed, part) draws one part's arguments, and reference() takes and returns one part's arrays. A program takes and returns all parts, laid end to end along the dimension named above; an argument that names none is the same for every part. Nothing has to cross between parts.
Inputs may be any that keep to these rules, and one draw needn't show every extreme that they name: `lower_block_columns`: entry k of block row (l * 8 + m) * 8 + p is either that row's own number (an empty slot) or ((l - 1) * 8 + m) * 8 + (p + d) mod 8 with d one of -1, 0, 1; the nonempty slots of a row have distinct d; rows with l = 0 have only empty slots. `upper_cols`: entry k of block row (l * 8 + m) * 8 + p is either that row's own number (an empty slot) or ((l + 1) * 8 + m) * 8 + (p + d) mod 8 with d one of -1, 0, 1; the nonempty slots of a row have distinct d; rows with l = 7 have only empty slots.
All inputs are finite; a program needn't handle non-finite values.
Results may differ from the reference program's by a relative error of at most 0.015.
Values may be sent and summed in bfloat16 or wider, within the bound.
A program may use at most 64 MiB of HBM per device.

```python
import math
import jax
import jax.numpy as jnp
from jax import lax

BLOCK = 128
SLOTS = 3
SIDES = 64
LEVELS = 8
ROW_DEV = 8
SPAN = 8


def pattern_columns(key, level_step, forced_row):
    dims_all = (LEVELS, ROW_DEV, SPAN, SLOTS)
    score_key, kept_key = jax.random.split(key)
    scores = jax.random.randint(score_key, dims_all, 0, 1 << 20) * 4 + lax.broadcasted_iota(jnp.int32, dims_all, 3)
    ranking = jnp.argsort(scores, axis=3, stable=True).astype(jnp.int32)
    offsets = ranking - 1
    levels = lax.broadcasted_iota(jnp.int32, dims_all, 0)
    places = lax.broadcasted_iota(jnp.int32, dims_all, 1)
    positions = lax.broadcasted_iota(jnp.int32, dims_all, 2)
    slot_ids = lax.broadcasted_iota(jnp.int32, dims_all, 3)
    numbers = (levels * ROW_DEV + places) * SPAN + positions
    target = ((levels + level_step) * ROW_DEV + places) * SPAN + (positions + offsets) % SPAN
    kept = jax.random.randint(kept_key, dims_all, 0, 4) > 0
    kept = kept & jnp.logical_not((numbers == forced_row) & (slot_ids == 0))
    inside = (levels + level_step >= 0) & (levels + level_step < LEVELS)
    return jnp.where(kept & inside, target, numbers).astype(jnp.int32)


def draw_lower_block_columns(key, part):
    return pattern_columns(jax.random.fold_in(key, 11), -1, LEVELS * ROW_DEV * SPAN - 1)


def draw_upper_cols(key, part):
    return pattern_columns(jax.random.fold_in(key, 23), 1, 0)


def draw_diag_inverse(key, part):
    dims_all = (LEVELS, ROW_DEV, SPAN, BLOCK, BLOCK)
    off_key, diagonal_key = jax.random.split(jax.random.fold_in(key, 37))
    off_part = jax.random.normal(off_key, dims_all, jnp.float32) * (0.6 / math.sqrt(BLOCK))
    diagonal_part = jax.random.uniform(diagonal_key, dims_all[:-1], jnp.float32, 0.7, 1.3)
    identity = (lax.broadcasted_iota(jnp.int32, (BLOCK, BLOCK), 0) == lax.broadcasted_iota(jnp.int32, (BLOCK, BLOCK), 1)).astype(jnp.float32)
    return (off_part * (1.0 - identity) + diagonal_part[..., None] * identity).astype(jnp.bfloat16)


def block_levels(stream_key, dims, cuts, least, largest):
    def one(axis_at, shards_of):
        draws = jax.random.uniform(jax.random.fold_in(jax.random.fold_in(stream_key, 6), axis_at), (shards_of,), jnp.float32, least / len(cuts), largest / len(cuts))
        return jnp.repeat(jnp.exp(draws), dims[axis_at] // shards_of).reshape((-1,) + (1,) * (len(dims) - axis_at - 1))

    level = one(*cuts[0])
    for cut in cuts[1:]:
        level = level * one(*cut)
    return level


def normal_values(stream_key, dims, spread, reach, pieces=(), kind=jnp.bfloat16):
    gain = block_levels(stream_key, dims, pieces, -0.22, 0.18) if pieces else 1.0
    result = jax.random.normal(stream_key, dims, jnp.float32) * spread * gain
    return jnp.minimum(jnp.maximum(result, -reach), reach).astype(kind)


def setup_inputs(seed: int = 0, part: int = 0) -> dict:
    streams_of = jax.random.split(jax.random.key(seed), 7)
    part_splits = jax.random.split(jax.random.fold_in(streams_of[6], part), 7)
    rhs = normal_values(part_splits[0], (LEVELS, ROW_DEV, SPAN, SIDES, BLOCK), 1.0, 6.0, ((2, 8),), jnp.float32)
    lower_tiles = normal_values(streams_of[1], (LEVELS, ROW_DEV, SPAN, SLOTS, BLOCK, BLOCK), (4 * BLOCK) ** -0.5, 0.25, ((2, 8),))
    lower_block_columns = draw_lower_block_columns(jax.random.fold_in(streams_of[6], 71), part)
    upper_tiles = normal_values(streams_of[3], (LEVELS, ROW_DEV, SPAN, SLOTS, BLOCK, BLOCK), (4 * BLOCK) ** -0.5, 0.25, ((2, 8),))
    upper_cols = draw_upper_cols(jax.random.fold_in(streams_of[6], 71), part)
    diag_inverse = draw_diag_inverse(jax.random.fold_in(streams_of[6], 71), part)
    return dict(rhs=rhs, lower_tiles=lower_tiles, lower_block_columns=lower_block_columns, upper_tiles=upper_tiles, upper_cols=upper_cols, diag_inverse=diag_inverse)


def level_products(solved, tile_collection, columns, numbers):
    chosen_entries = solved[columns].astype(jnp.float32)
    present = (columns != numbers[:, None]).astype(jnp.float32)
    chosen_entries = chosen_entries * present[:, :, None, None]
    return jnp.einsum("rksb,rkab->rsa", chosen_entries, tile_collection.astype(jnp.float32))


def reference(rhs, lower_tiles, lower_block_columns, upper_tiles, upper_cols, diag_inverse):
    per_level = ROW_DEV * SPAN
    row_total = LEVELS * per_level
    side_rows = rhs.reshape(LEVELS, per_level, SIDES, BLOCK)
    lower_tile_group = lower_tiles.reshape(LEVELS, per_level, SLOTS, BLOCK, BLOCK)
    lower_index = lower_block_columns.reshape(LEVELS, per_level, SLOTS)
    upper_set = upper_tiles.reshape(LEVELS, per_level, SLOTS, BLOCK, BLOCK)
    upper_index = upper_cols.reshape(LEVELS, per_level, SLOTS)
    inverse = diag_inverse.reshape(LEVELS, per_level, BLOCK, BLOCK)
    numbers_all = jnp.arange(row_total, dtype=jnp.int32).reshape(LEVELS, per_level)

    def forward(level_id, solved):
        numbers = numbers_all[level_id]
        products = level_products(solved, lower_tile_group[level_id], lower_index[level_id], numbers)
        solved_now = lax.optimization_barrier((side_rows[level_id] - products).astype(jnp.bfloat16))
        offset_row = (level_id * per_level).astype(jnp.int32)
        return lax.dynamic_update_slice_in_dim(solved, solved_now, offset_row, 0)

    forward_rows = lax.fori_loop(0, LEVELS, forward, jnp.zeros((row_total, SIDES, BLOCK), jnp.bfloat16))

    def backward(countdown, finished):
        level_id = LEVELS - 1 - countdown
        numbers = numbers_all[level_id]
        products = level_products(finished, upper_set[level_id], upper_index[level_id], numbers)
        offset_row = (level_id * per_level).astype(jnp.int32)
        current = lax.dynamic_slice_in_dim(forward_rows, offset_row, per_level, 0).astype(jnp.float32)
        summed_terms = lax.optimization_barrier((current - products).astype(jnp.bfloat16))
        solved_now = jnp.einsum("rsb,rab->rsa", summed_terms.astype(jnp.float32), inverse[level_id].astype(jnp.float32)).astype(jnp.bfloat16)
        return lax.dynamic_update_slice_in_dim(finished, lax.optimization_barrier(solved_now), offset_row, 0)

    finished = lax.fori_loop(0, LEVELS, backward, jnp.zeros((row_total, SIDES, BLOCK), jnp.bfloat16))
    return finished.reshape(LEVELS, ROW_DEV, SPAN, SIDES, BLOCK)
```

```python
import functools

import jax
import jax.numpy as jnp
from jax import lax
from jax.experimental import pallas as pl
from jax.experimental.pallas import tpu as pltpu
from jax.sharding import PartitionSpec as P

MESH = pl.DeviceIdType.MESH
CHUNKS = 4


def product(x, tile):
    return lax.dot_general(x, tile, (((1,), (1,)), ((), ())), preferred_element_type=jnp.float32)


def sweep_kernel(
    n,
    chunks,
    lower_cols,
    upper_cols,
    rhs,
    lower,
    upper,
    inverse,
    out,
    rhs_v,
    lower_v,
    upper_v,
    inverse_v,
    y,
    x,
    from_left,
    from_right,
    load_sem,
    store_sem,
    send_sem,
    recv_sem,
):
    levels, rows, sides, block = rhs.shape
    slots = lower.shape[2]
    step = rows // chunks
    me = lax.axis_index("blk")
    left = lax.rem(me + n - 1, n)
    right = lax.rem(me + 1, n)

    def load(kind, level):
        source, target = ((rhs, rhs_v), (lower, lower_v), (upper, upper_v), (inverse, inverse_v))[kind]
        return pltpu.make_async_copy(source.at[level], target.at[level], load_sem.at[kind, level])

    def start_forward(level, carry):
        load(0, level).start()
        load(1, level).start()
        return carry

    def start_backward(i, carry):
        level = levels - 2 - i
        load(3, level).start()
        load(2, level).start()
        return carry

    load(0, 0).start()
    barrier = pltpu.get_barrier_semaphore()
    for neighbour in (left, right):
        pl.semaphore_signal(barrier, inc=1, device_id={"blk": neighbour}, device_id_type=MESH)
    lax.fori_loop(1, levels, start_forward, 0)
    load(3, levels - 1).start()
    lax.fori_loop(0, levels - 1, start_backward, 0)

    def exchange(source, sweep, level, c):
        part = pl.ds(c * step, step)
        to_right = pltpu.make_async_remote_copy(
            src_ref=source.at[level, part],
            dst_ref=from_left.at[sweep, level, part],
            send_sem=send_sem.at[sweep, level, c, 0],
            recv_sem=recv_sem.at[sweep, level, c, 0],
            device_id={"blk": right},
            device_id_type=MESH,
        )
        to_left = pltpu.make_async_remote_copy(
            src_ref=source.at[level, part],
            dst_ref=from_right.at[sweep, level, part],
            send_sem=send_sem.at[sweep, level, c, 1],
            recv_sem=recv_sem.at[sweep, level, c, 1],
            device_id={"blk": left},
            device_id_type=MESH,
        )
        return to_right, to_left

    def terms(acc, cols, tiles, centre, sweep, level, source, m):
        base = (source * rows + m) * n
        low = from_left[sweep, source, m]
        mid = centre[source, m]
        high = from_right[sweep, source, m]
        for k in range(slots):
            column = cols[(level * rows + m) * slots + k]
            chosen = lax.select(column == base + right, high, jnp.zeros_like(high))
            chosen = lax.select(column == base + me, mid, chosen)
            chosen = lax.select(column == base + left, low, chosen)
            acc = acc - product(chosen, tiles[level, m, k])
        return acc

    load(0, 0).wait()
    y[0] = rhs_v[0].astype(jnp.bfloat16)
    pl.semaphore_wait(barrier, 2)
    for c in range(chunks):
        for copy in exchange(y, 0, 0, c):
            copy.start()

    def forward(level, carry):
        load(0, level).wait()
        load(1, level).wait()
        for c in range(chunks):
            for copy in exchange(y, 0, level - 1, c):
                copy.wait_recv()
            for m in range(c * step, (c + 1) * step):
                acc = terms(rhs_v[level, m], lower_cols, lower_v, y, 0, level, level - 1, m)
                y[level, m] = acc.astype(jnp.bfloat16)

            @pl.when(level < levels - 1)
            def _():
                for copy in exchange(y, 0, level, c):
                    copy.start()

        return carry

    lax.fori_loop(1, levels, forward, 0)

    last = levels - 1
    load(3, last).wait()
    for c in range(chunks):
        for m in range(c * step, (c + 1) * step):
            x[last, m] = product(y[last, m], inverse_v[last, m]).astype(jnp.bfloat16)
        for copy in exchange(x, 1, last, c):
            copy.start()

    def store(level):
        return pltpu.make_async_copy(x.at[level], out.at[level], store_sem.at[level])

    store(last).start()

    def backward(i, carry):
        level = last - 1 - i
        load(3, level).wait()
        load(2, level).wait()
        for c in range(chunks):
            for copy in exchange(x, 1, level + 1, c):
                copy.wait_recv()
            for m in range(c * step, (c + 1) * step):
                acc = terms(
                    y[level, m].astype(jnp.float32), upper_cols, upper_v, x, 1, level, level + 1, m
                )
                w = acc.astype(jnp.bfloat16)
                x[level, m] = product(w, inverse_v[level, m]).astype(jnp.bfloat16)

            @pl.when(level > 0)
            def _():
                for copy in exchange(x, 1, level, c):
                    copy.start()

        store(level).start()
        return carry

    lax.fori_loop(0, last, backward, 0)

    def finish(i, carry):
        for c in range(chunks):
            for copy in exchange(y, 0, i, c) + exchange(x, 1, i + 1, c):
                copy.wait_send()
        store(i).wait()
        return carry

    lax.fori_loop(0, last, finish, 0)
    store(last).wait()


def on_device(n, rhs, lower_tiles, lower_block_columns, upper_tiles, upper_cols, diag_inverse):
    rhs = rhs[:, :, 0]
    lower = lower_tiles[:, :, 0]
    upper = upper_tiles[:, :, 0]
    inverse = diag_inverse[:, :, 0]
    levels, rows, sides, block = rhs.shape
    chunks = CHUNKS if rows % CHUNKS == 0 else 1
    halo = pltpu.VMEM((2, levels, rows, sides, block), jnp.bfloat16)
    own = pltpu.VMEM((levels, rows, sides, block), jnp.bfloat16)
    any_space = pl.BlockSpec(memory_space=pl.ANY)
    small = pl.BlockSpec(memory_space=pltpu.SMEM)
    result = pl.pallas_call(
        functools.partial(sweep_kernel, n, chunks),
        out_shape=jax.ShapeDtypeStruct(rhs.shape, jnp.bfloat16),
        in_specs=[small, small, any_space, any_space, any_space, any_space],
        out_specs=any_space,
        scratch_shapes=[
            pltpu.VMEM(rhs.shape, rhs.dtype),
            pltpu.VMEM(lower.shape, lower.dtype),
            pltpu.VMEM(upper.shape, upper.dtype),
            pltpu.VMEM(inverse.shape, inverse.dtype),
            own,
            own,
            halo,
            halo,
            pltpu.SemaphoreType.DMA((4, levels)),
            pltpu.SemaphoreType.DMA((levels,)),
            pltpu.SemaphoreType.DMA((2, levels, chunks, 2)),
            pltpu.SemaphoreType.DMA((2, levels, chunks, 2)),
        ],
        compiler_params=pltpu.CompilerParams(collective_id=0, has_side_effects=True),
    )(
        lower_block_columns.reshape(-1),
        upper_cols.reshape(-1),
        rhs,
        lower,
        upper,
        inverse,
    )
    return result[:, :, None]


def solution(mesh):
    return jax.shard_map(
        functools.partial(on_device, mesh.shape["blk"]),
        mesh=mesh,
        in_specs=(
            P(None, None, "blk", "rhs", None),
            P(None, None, "blk", None, None, None),
            P(None, None, "blk", None),
            P(None, None, "blk", None, None, None),
            P(None, None, "blk", None),
            P(None, None, "blk", None, None),
        ),
        out_specs=P(None, None, "blk", "rhs", None),
        check_vma=False,
    )
```

```python
import functools

import jax
import jax.numpy as jnp
from jax import lax
from jax.experimental import pallas as pl
from jax.experimental.pallas import tpu as pltpu
from jax.sharding import PartitionSpec as P

MESH = pl.DeviceIdType.MESH
CHUNKS = 4
LOOK = 2


def product(x, tile):
    return lax.dot_general(x, tile, (((1,), (1,)), ((), ())), preferred_element_type=jnp.float32)


def sweep_kernel(
    n,
    chunks,
    lower_cols,
    upper_cols,
    rhs,
    lower,
    upper,
    inverse,
    out,
    rhs_v,
    lower_v,
    upper_v,
    inverse_v,
    y,
    x,
    from_near,
    from_far,
    load_sem,
    store_sem,
    send_sem,
    recv_sem,
):
    levels, rows, sides, block = rhs.shape
    slots = lower.shape[2]
    step = rows // chunks
    last = levels - 1
    me = lax.axis_index("blk")
    odd = lax.rem(me, 2)
    near = me + 1 - 2 * odd
    far = lax.rem(me + 2 * odd + n - 1, n)
    onward = me + 2 - 4 * odd
    forwards = (onward >= 0) & (onward < n)
    ends = (me == 0) | (me == n - 1)
    feeder = lax.select(ends, far, me - 2 + 4 * odd)

    def load(kind, level):
        source, target = ((rhs, rhs_v), (lower, lower_v), (upper, upper_v), (inverse, inverse_v))[kind]
        return pltpu.make_async_copy(source.at[level], target.at[level], load_sem.at[kind, level])

    def start_forward(level, carry):
        load(0, level).start()
        load(1, level).start()
        return carry

    def start_backward(i, carry):
        level = levels - 2 - i
        load(3, level).start()
        load(2, level).start()
        return carry

    load(0, 0).start()
    barrier = pltpu.get_barrier_semaphore()
    for device in (near, feeder):
        pl.semaphore_signal(barrier, inc=1, device_id={"blk": device}, device_id_type=MESH)
    lax.fori_loop(1, levels, start_forward, 0)
    load(3, levels - 1).start()
    lax.fori_loop(0, levels - 1, start_backward, 0)

    def remote(source, target, sweep, level, c, kind, device):
        part = pl.ds(c * step, step)
        return pltpu.make_async_remote_copy(
            src_ref=source.at[level, part] if kind != 1 else source.at[sweep, level, part],
            dst_ref=target.at[sweep, level, part],
            send_sem=send_sem.at[sweep, level, c, kind],
            recv_sem=recv_sem.at[sweep, level, c, min(kind, 1)],
            device_id={"blk": device},
            device_id_type=MESH,
        )

    def to_near(own, sweep, level, c):
        return remote(own, from_near, sweep, level, c, 0, near)

    def to_onward(sweep, level, c):
        return remote(from_near, from_far, sweep, level, c, 1, onward)

    def to_far(own, sweep, level, c):
        return remote(own, from_far, sweep, level, c, 2, far)

    def send(own, sweep, level, c):
        @pl.when(ends)
        def _():
            to_far(own, sweep, level, c).start()

        to_near(own, sweep, level, c).start()

    def relay(own, sweep, level, c):
        to_near(own, sweep, level, c).wait_recv()

        @pl.when(forwards)
        def _():
            to_onward(sweep, level, c).start()

    def ahead(own, sweep, level, source, c):
        if c + LOOK < chunks:
            relay(own, sweep, source, c + LOOK)
        else:

            @pl.when((level > 0) & (level < last))
            def _():
                relay(own, sweep, level, c + LOOK - chunks)

    def terms(acc, cols, tiles, centre, sweep, level, source, m):
        base = (source * rows + m) * n
        side = from_near[sweep, source, m]
        mid = centre[source, m]
        other = from_far[sweep, source, m]
        for k in range(slots):
            column = cols[level, k, 0, m]
            chosen = lax.select(column == base + far, other, jnp.zeros_like(other))
            chosen = lax.select(column == base + me, mid, chosen)
            chosen = lax.select(column == base + near, side, chosen)
            acc = acc - product(chosen, tiles[level, m, k])
        return acc

    load(0, 0).wait()
    y[0] = rhs_v[0].astype(jnp.bfloat16)
    pl.semaphore_wait(barrier, 1 + forwards.astype(jnp.int32) + ends.astype(jnp.int32))
    for c in range(chunks):
        send(y, 0, 0, c)
    for c in range(LOOK):
        relay(y, 0, 0, c)

    def forward(level, carry):
        load(0, level).wait()
        load(1, level).wait()
        for c in range(chunks):
            ahead(y, 0, level, level - 1, c)
            to_far(y, 0, level - 1, c).wait_recv()
            for m in range(c * step, (c + 1) * step):
                acc = terms(rhs_v[level, m], lower_cols, lower_v, y, 0, level, level - 1, m)
                y[level, m] = acc.astype(jnp.bfloat16)

            @pl.when(level < levels - 1)
            def _():
                send(y, 0, level, c)

        return carry

    lax.fori_loop(1, levels, forward, 0)

    load(3, last).wait()
    for c in range(chunks):
        for m in range(c * step, (c + 1) * step):
            x[last, m] = product(y[last, m], inverse_v[last, m]).astype(jnp.bfloat16)
        send(x, 1, last, c)
    for c in range(LOOK):
        relay(x, 1, last, c)

    def store(level):
        return pltpu.make_async_copy(x.at[level], out.at[level], store_sem.at[level])

    store(last).start()

    def backward(i, carry):
        level = last - 1 - i
        load(3, level).wait()
        load(2, level).wait()
        for c in range(chunks):
            ahead(x, 1, level, level + 1, c)
            to_far(x, 1, level + 1, c).wait_recv()
            for m in range(c * step, (c + 1) * step):
                acc = terms(
                    y[level, m].astype(jnp.float32), upper_cols, upper_v, x, 1, level, level + 1, m
                )
                w = acc.astype(jnp.bfloat16)
                x[level, m] = product(w, inverse_v[level, m]).astype(jnp.bfloat16)

            @pl.when(level > 0)
            def _():
                send(x, 1, level, c)

        store(level).start()
        return carry

    lax.fori_loop(0, last, backward, 0)

    def finish(i, carry):
        for c in range(chunks):
            for own, sweep, level in ((y, 0, i), (x, 1, i + 1)):
                to_near(own, sweep, level, c).wait_send()

                @pl.when(forwards)
                def _():
                    to_onward(sweep, level, c).wait_send()

                @pl.when(ends)
                def _():
                    to_far(own, sweep, level, c).wait_send()

        store(i).wait()
        return carry

    lax.fori_loop(0, last, finish, 0)
    store(last).wait()


def on_device(n, rhs, lower_tiles, lower_block_columns, upper_tiles, upper_cols, diag_inverse):
    rhs = rhs[:, :, 0]
    lower = lower_tiles[:, :, 0]
    upper = upper_tiles[:, :, 0]
    inverse = diag_inverse[:, :, 0]
    levels, rows, sides, block = rhs.shape
    chunks = CHUNKS if rows % CHUNKS == 0 else 1
    halo = pltpu.VMEM((2, levels, rows, sides, block), jnp.bfloat16)
    own = pltpu.VMEM((levels, rows, sides, block), jnp.bfloat16)
    any_space = pl.BlockSpec(memory_space=pl.ANY)
    small = pl.BlockSpec(memory_space=pltpu.SMEM)
    result = pl.pallas_call(
        functools.partial(sweep_kernel, n, chunks),
        out_shape=jax.ShapeDtypeStruct(rhs.shape, jnp.bfloat16),
        in_specs=[small, small, any_space, any_space, any_space, any_space],
        out_specs=any_space,
        scratch_shapes=[
            pltpu.VMEM(rhs.shape, rhs.dtype),
            pltpu.VMEM(lower.shape, lower.dtype),
            pltpu.VMEM(upper.shape, upper.dtype),
            pltpu.VMEM(inverse.shape, inverse.dtype),
            own,
            own,
            halo,
            halo,
            pltpu.SemaphoreType.DMA((4, levels)),
            pltpu.SemaphoreType.DMA((levels,)),
            pltpu.SemaphoreType.DMA((2, levels, chunks, 3)),
            pltpu.SemaphoreType.DMA((2, levels, chunks, 2)),
        ],
        compiler_params=pltpu.CompilerParams(collective_id=0, has_side_effects=True),
    )(
        lower_block_columns.transpose(0, 3, 2, 1),
        upper_cols.transpose(0, 3, 2, 1),
        rhs,
        lower,
        upper,
        inverse,
    )
    return result[:, :, None]


def solution(mesh):
    return jax.shard_map(
        functools.partial(on_device, mesh.shape["blk"]),
        mesh=mesh,
        in_specs=(
            P(None, None, "blk", "rhs", None),
            P(None, None, "blk", None, None, None),
            P(None, None, "blk", None),
            P(None, None, "blk", None, None, None),
            P(None, None, "blk", None),
            P(None, None, "blk", None, None),
        ),
        out_specs=P(None, None, "blk", "rhs", None),
        check_vma=False,
    )
```

```python
import functools

import jax
import jax.numpy as jnp
from jax import lax
from jax.experimental import pallas as pl
from jax.experimental.pallas import tpu as pltpu
from jax.sharding import PartitionSpec as P

MESH = pl.DeviceIdType.MESH
CHUNKS = 8
RELAYED = 1


def product(x, tile):
    return lax.dot_general(x, tile, (((1,), (1,)), ((), ())), preferred_element_type=jnp.float32)


def sweep_kernel(
    n,
    chunks,
    lower_cols,
    upper_cols,
    rhs,
    lower,
    upper,
    inverse,
    out,
    rhs_v,
    lower_v,
    upper_v,
    inverse_v,
    y,
    x,
    from_near,
    from_far,
    load_sem,
    store_sem,
    send_sem,
    recv_sem,
):
    levels, rows, sides, block = rhs.shape
    slots = lower.shape[2]
    step = rows // chunks
    last = levels - 1
    me = lax.axis_index("blk")
    odd = lax.rem(me, 2)
    near = me + 1 - 2 * odd
    far = lax.rem(me + 2 * odd + n - 1, n)
    onward = lax.rem(me + 2 - 4 * odd + n, n)
    feeder = lax.rem(me - 2 + 4 * odd + n, n)

    def load(kind, level):
        source, target = ((rhs, rhs_v), (lower, lower_v), (upper, upper_v), (inverse, inverse_v))[kind]
        return pltpu.make_async_copy(source.at[level], target.at[level], load_sem.at[kind, level])

    def start_forward(level, carry):
        load(0, level).start()
        load(1, level).start()
        return carry

    def start_backward(i, carry):
        level = levels - 2 - i
        load(3, level).start()
        load(2, level).start()
        return carry

    load(0, 0).start()
    barrier = pltpu.get_barrier_semaphore()
    for device in (near, far, feeder) if RELAYED else (near, far):
        pl.semaphore_signal(barrier, inc=1, device_id={"blk": device}, device_id_type=MESH)
    lax.fori_loop(1, levels, start_forward, 0)
    load(3, levels - 1).start()
    lax.fori_loop(0, levels - 1, start_backward, 0)

    def group(turn, j):
        return lax.rem(turn * RELAYED + j, chunks) * step

    def remote(source, target, sweep, level, turn, j, kind, device):
        return pltpu.make_async_remote_copy(
            src_ref=source.at[level, pl.ds(group(turn, j), step)],
            dst_ref=target.at[sweep, level, pl.ds(group(turn, j), step)],
            send_sem=send_sem.at[sweep, level, j, kind],
            recv_sem=recv_sem.at[sweep, level, j, kind],
            device_id={"blk": device},
            device_id_type=MESH,
        )

    def to_near(own, sweep, level, turn, j):
        return remote(own, from_near, sweep, level, turn, j, 0, near)

    def to_far(own, sweep, level, turn, j):
        if j < RELAYED:
            return remote(from_near.at[sweep], from_far, sweep, level, turn, j, 1, onward)
        return remote(own, from_far, sweep, level, turn, j, 1, far)

    def send(own, sweep, level, turn, j):
        if j >= RELAYED:
            to_far(own, sweep, level, turn, j).start()
        to_near(own, sweep, level, turn, j).start()

    def relay(own, sweep, level, turn):
        for j in range(RELAYED):
            to_near(own, sweep, level, turn, j).wait_recv()
            to_far(own, sweep, level, turn, j).start()

    def receive(own, sweep, level, turn, j):
        if j >= RELAYED:
            to_near(own, sweep, level, turn, j).wait_recv()
        to_far(own, sweep, level, turn, j).wait_recv()

    def terms(acc, cols, tiles, centre, sweep, level, source, m):
        base = (source * rows + m) * n
        side = from_near[sweep, source, m]
        mid = centre[source, m]
        other = from_far[sweep, source, m]
        for k in range(slots):
            column = cols[level, k, 0, m]
            chosen = lax.select(column == base + far, other, jnp.zeros_like(other))
            chosen = lax.select(column == base + me, mid, chosen)
            chosen = lax.select(column == base + near, side, chosen)
            acc = acc - product(chosen, tiles[level, m, k])
        return acc

    load(0, 0).wait()
    y[0] = rhs_v[0].astype(jnp.bfloat16)
    pl.semaphore_wait(barrier, 3 if RELAYED else 2)
    for j in range(chunks):
        send(y, 0, 0, 0, j)
    relay(y, 0, 0, 0)

    def forward(level, carry):
        load(0, level).wait()
        load(1, level).wait()
        for j in range(chunks):
            receive(y, 0, level - 1, level - 1, (j + RELAYED) % chunks)
            for i in range(step):
                m = group(level, j) + i
                acc = terms(rhs_v[level, m], lower_cols, lower_v, y, 0, level, level - 1, m)
                y[level, m] = acc.astype(jnp.bfloat16)

            @pl.when(level < last)
            def _():
                send(y, 0, level, level, j)

        @pl.when(level < last)
        def _():
            relay(y, 0, level, level)

        return carry

    lax.fori_loop(1, levels, forward, 0)

    def store(level):
        return pltpu.make_async_copy(x.at[level], out.at[level], store_sem.at[level])

    load(3, last).wait()
    for j in range(chunks):
        for i in range(step):
            m = group(0, j) + i
            x[last, m] = product(y[last, m], inverse_v[last, m]).astype(jnp.bfloat16)
        send(x, 1, last, 0, j)
    store(last).start()
    relay(x, 1, last, 0)

    def backward(turn, carry):
        level = last - turn
        load(3, level).wait()
        load(2, level).wait()
        for j in range(chunks):
            receive(x, 1, level + 1, turn - 1, (j + RELAYED) % chunks)
            for i in range(step):
                m = group(turn, j) + i
                acc = terms(
                    y[level, m].astype(jnp.float32), upper_cols, upper_v, x, 1, level, level + 1, m
                )
                w = acc.astype(jnp.bfloat16)
                x[level, m] = product(w, inverse_v[level, m]).astype(jnp.bfloat16)

            @pl.when(level > 0)
            def _():
                send(x, 1, level, turn, j)

        store(level).start()

        @pl.when(level > 0)
        def _():
            relay(x, 1, level, turn)

        return carry

    lax.fori_loop(1, levels, backward, 0)

    def finish(turn, carry):
        for j in range(chunks):
            for own, sweep, level in ((y, 0, turn), (x, 1, last - turn)):
                to_near(own, sweep, level, turn, j).wait_send()
                to_far(own, sweep, level, turn, j).wait_send()
        store(turn).wait()
        return carry

    lax.fori_loop(0, last, finish, 0)
    store(last).wait()


def on_device(n, rhs, lower_tiles, lower_block_columns, upper_tiles, upper_cols, diag_inverse):
    rhs = rhs[:, :, 0]
    lower = lower_tiles[:, :, 0]
    upper = upper_tiles[:, :, 0]
    inverse = diag_inverse[:, :, 0]
    levels, rows, sides, block = rhs.shape
    chunks = CHUNKS if rows % CHUNKS == 0 else 1
    halo = pltpu.VMEM((2, levels, rows, sides, block), jnp.bfloat16)
    own = pltpu.VMEM((levels, rows, sides, block), jnp.bfloat16)
    any_space = pl.BlockSpec(memory_space=pl.ANY)
    small = pl.BlockSpec(memory_space=pltpu.SMEM)
    result = pl.pallas_call(
        functools.partial(sweep_kernel, n, chunks),
        out_shape=jax.ShapeDtypeStruct(rhs.shape, jnp.bfloat16),
        in_specs=[small, small, any_space, any_space, any_space, any_space],
        out_specs=any_space,
        scratch_shapes=[
            pltpu.VMEM(rhs.shape, rhs.dtype),
            pltpu.VMEM(lower.shape, lower.dtype),
            pltpu.VMEM(upper.shape, upper.dtype),
            pltpu.VMEM(inverse.shape, inverse.dtype),
            own,
            own,
            halo,
            halo,
            pltpu.SemaphoreType.DMA((4, levels)),
            pltpu.SemaphoreType.DMA((levels,)),
            pltpu.SemaphoreType.DMA((2, levels, chunks, 2)),
            pltpu.SemaphoreType.DMA((2, levels, chunks, 2)),
        ],
        compiler_params=pltpu.CompilerParams(collective_id=0, has_side_effects=True),
    )(
        lower_block_columns.transpose(0, 3, 2, 1),
        upper_cols.transpose(0, 3, 2, 1),
        rhs,
        lower,
        upper,
        inverse,
    )
    return result[:, :, None]


def solution(mesh):
    return jax.shard_map(
        functools.partial(on_device, mesh.shape["blk"]),
        mesh=mesh,
        in_specs=(
            P(None, None, "blk", "rhs", None),
            P(None, None, "blk", None, None, None),
            P(None, None, "blk", None),
            P(None, None, "blk", None, None, None),
            P(None, None, "blk", None),
            P(None, None, "blk", None, None),
        ),
        out_specs=P(None, None, "blk", "rhs", None),
        check_vma=False,
    )
```

```python
import functools

import jax
import jax.numpy as jnp
from jax import lax
from jax.experimental import pallas as pl
from jax.experimental.pallas import tpu as pltpu
from jax.sharding import PartitionSpec as P

MESH = pl.DeviceIdType.MESH
CHUNKS = 8
VMEM_LIMIT = 52 * 2**20
RELAYED = 1


def product(x, tile):
    return lax.dot_general(x, tile, (((1,), (1,)), ((), ())), preferred_element_type=jnp.float32)


def sweep_kernel(
    n,
    chunks,
    lower_cols,
    upper_cols,
    rhs,
    lower,
    upper,
    inverse,
    out,
    rhs_v,
    lower_v,
    upper_v,
    inverse_v,
    y,
    x,
    from_near,
    from_far,
    load_sem,
    store_sem,
    send_sem,
    recv_sem,
):
    levels, rows, sides, block = rhs.shape
    slots = lower.shape[2]
    step = rows // chunks
    last = levels - 1
    me = lax.axis_index("blk")
    odd = lax.rem(me, 2)
    near = me + 1 - 2 * odd
    far = lax.rem(me + 2 * odd + n - 1, n)
    onward = lax.rem(me + 2 - 4 * odd + n, n)
    feeder = lax.rem(me - 2 + 4 * odd + n, n)

    def load(kind, level):
        source, target = ((rhs, rhs_v), (lower, lower_v), (upper, upper_v), (inverse, inverse_v))[kind]
        return pltpu.make_async_copy(source.at[level], target.at[level], load_sem.at[kind, level])

    def start_forward(level, carry):
        load(0, level).start()
        load(1, level).start()
        return carry

    def start_backward(i, carry):
        level = levels - 2 - i
        load(3, level).start()
        load(2, level).start()
        return carry

    load(0, 0).start()
    barrier = pltpu.get_barrier_semaphore()
    for device in (near, far, feeder) if RELAYED else (near, far):
        pl.semaphore_signal(barrier, inc=1, device_id={"blk": device}, device_id_type=MESH)
    lax.fori_loop(1, levels, start_forward, 0)
    load(3, levels - 1).start()
    lax.fori_loop(0, levels - 1, start_backward, 0)

    def group(turn, j):
        return lax.rem(turn * RELAYED + j, chunks) * step

    def remote(source, target, sweep, level, turn, j, kind, device):
        return pltpu.make_async_remote_copy(
            src_ref=source.at[level, pl.ds(group(turn, j), step)],
            dst_ref=target.at[sweep, level, pl.ds(group(turn, j), step)],
            send_sem=send_sem.at[sweep, level, j, kind],
            recv_sem=recv_sem.at[sweep, level, j, kind],
            device_id={"blk": device},
            device_id_type=MESH,
        )

    def to_near(own, sweep, level, turn, j):
        return remote(own, from_near, sweep, level, turn, j, 0, near)

    def to_far(own, sweep, level, turn, j):
        if j < RELAYED:
            return remote(from_near.at[sweep], from_far, sweep, level, turn, j, 1, onward)
        return remote(own, from_far, sweep, level, turn, j, 1, far)

    def send(own, sweep, level, turn, j):
        to_near(own, sweep, level, turn, j).start()
        if j >= RELAYED:
            to_far(own, sweep, level, turn, j).start()

    def relay(own, sweep, level, turn):
        for j in range(RELAYED):
            to_near(own, sweep, level, turn, j).wait_recv()
            to_far(own, sweep, level, turn, j).start()

    def receive(own, sweep, level, turn, j):
        if j >= RELAYED:
            to_near(own, sweep, level, turn, j).wait_recv()
        to_far(own, sweep, level, turn, j).wait_recv()

    def terms(acc, cols, tiles, centre, sweep, level, source, m):
        base = (source * rows + m) * n
        side = from_near[sweep, source, m]
        mid = centre[source, m]
        other = from_far[sweep, source, m]
        for k in range(slots):
            column = cols[level, k, 0, m]
            chosen = lax.select(column == base + far, other, jnp.zeros_like(other))
            chosen = lax.select(column == base + me, mid, chosen)
            chosen = lax.select(column == base + near, side, chosen)
            acc = acc - product(chosen, tiles[level, m, k])
        return acc

    load(0, 0).wait()
    y[0] = rhs_v[0].astype(jnp.bfloat16)
    pl.semaphore_wait(barrier, 3 if RELAYED else 2)
    for j in range(chunks):
        send(y, 0, 0, 0, j)
    relay(y, 0, 0, 0)

    def forward(level, carry):
        load(0, level).wait()
        load(1, level).wait()
        for j in range(chunks):
            receive(y, 0, level - 1, level - 1, (j + RELAYED) % chunks)
            for i in range(step):
                m = group(level, j) + i
                acc = terms(rhs_v[level, m], lower_cols, lower_v, y, 0, level, level - 1, m)
                y[level, m] = acc.astype(jnp.bfloat16)

            @pl.when(level < last)
            def _():
                send(y, 0, level, level, j)

        @pl.when(level < last)
        def _():
            relay(y, 0, level, level)

        return carry

    lax.fori_loop(1, levels, forward, 0)

    def store(level):
        return pltpu.make_async_copy(x.at[level], out.at[level], store_sem.at[level])

    load(3, last).wait()
    for j in range(chunks):
        for i in range(step):
            m = group(0, j) + i
            x[last, m] = product(y[last, m], inverse_v[last, m]).astype(jnp.bfloat16)
        send(x, 1, last, 0, j)
    store(last).start()
    relay(x, 1, last, 0)

    def backward(turn, carry):
        level = last - turn
        load(3, level).wait()
        load(2, level).wait()
        for j in range(chunks):
            receive(x, 1, level + 1, turn - 1, (j + RELAYED) % chunks)
            for i in range(step):
                m = group(turn, j) + i
                acc = terms(
                    y[level, m].astype(jnp.float32), upper_cols, upper_v, x, 1, level, level + 1, m
                )
                w = acc.astype(jnp.bfloat16)
                x[level, m] = product(w, inverse_v[level, m]).astype(jnp.bfloat16)

            @pl.when(level > 0)
            def _():
                send(x, 1, level, turn, j)

        store(level).start()

        @pl.when(level > 0)
        def _():
            relay(x, 1, level, turn)

        return carry

    lax.fori_loop(1, levels, backward, 0)

    def finish(turn, carry):
        for j in range(chunks):
            for own, sweep, level in ((y, 0, turn), (x, 1, last - turn)):
                to_near(own, sweep, level, turn, j).wait_send()
                to_far(own, sweep, level, turn, j).wait_send()
        store(turn).wait()
        return carry

    lax.fori_loop(0, last, finish, 0)
    store(last).wait()


def on_device(n, rhs, lower_tiles, lower_block_columns, upper_tiles, upper_cols, diag_inverse):
    rhs = rhs[:, :, 0]
    lower = lower_tiles[:, :, 0]
    upper = upper_tiles[:, :, 0]
    inverse = diag_inverse[:, :, 0]
    levels, rows, sides, block = rhs.shape
    chunks = CHUNKS if rows % CHUNKS == 0 else 1
    halo = pltpu.VMEM((2, levels, rows, sides, block), jnp.bfloat16)
    own = pltpu.VMEM((levels, rows, sides, block), jnp.bfloat16)
    any_space = pl.BlockSpec(memory_space=pl.ANY)
    small = pl.BlockSpec(memory_space=pltpu.SMEM)
    result = pl.pallas_call(
        functools.partial(sweep_kernel, n, chunks),
        out_shape=jax.ShapeDtypeStruct(rhs.shape, jnp.bfloat16),
        in_specs=[small, small, any_space, any_space, any_space, any_space],
        out_specs=any_space,
        scratch_shapes=[
            pltpu.VMEM(rhs.shape, rhs.dtype),
            pltpu.VMEM(lower.shape, lower.dtype),
            pltpu.VMEM(upper.shape, upper.dtype),
            pltpu.VMEM(inverse.shape, inverse.dtype),
            own,
            own,
            halo,
            halo,
            pltpu.SemaphoreType.DMA((4, levels)),
            pltpu.SemaphoreType.DMA((levels,)),
            pltpu.SemaphoreType.DMA((2, levels, chunks, 2)),
            pltpu.SemaphoreType.DMA((2, levels, chunks, 2)),
        ],
        compiler_params=pltpu.CompilerParams(collective_id=0, has_side_effects=True, vmem_limit_bytes=VMEM_LIMIT),
    )(
        lower_block_columns.transpose(0, 3, 2, 1),
        upper_cols.transpose(0, 3, 2, 1),
        rhs,
        lower,
        upper,
        inverse,
    )
    return result[:, :, None]


def solution(mesh):
    return jax.shard_map(
        functools.partial(on_device, mesh.shape["blk"]),
        mesh=mesh,
        in_specs=(
            P(None, None, "blk", "rhs", None),
            P(None, None, "blk", None, None, None),
            P(None, None, "blk", None),
            P(None, None, "blk", None, None, None),
            P(None, None, "blk", None),
            P(None, None, "blk", None, None),
        ),
        out_specs=P(None, None, "blk", "rhs", None),
        check_vma=False,
    )
```
